32 devices in a mesh: row: 4 (over z), col: 8 (over y, x, core).
Axes of the slice: x: 2, y: 2, z: 4, core: 2. Of those that a mesh axis runs over, the one named last changes fastest.
Arguments:
- matrix_tiles: float32 [4, 8, 16, 512, 512], P('row', 'col'), may hold values from -0.25 to 0.25
- tile_rows: int32 [4, 8, 16], P('row', 'col'), may hold values from 0 to 63, as said below
- tile_columns: int32 [4, 8, 16], P('row', 'col'), may hold values from 0 to 31, as said below
- tile_counts: int32 [4, 8], P('row', 'col'), may hold values from 8 to 16, as said below
- primal_iter: float32 [2, 131072], P(None, ('col', 'row')), may hold values from -6 to 6
- dual_iter: float32 [2, 131072], P(None, ('row', 'col')), may hold values from -6 to 6
- requirement: float32 [131072], P('row'), may hold values from -68 to 68
- constraint_kind: int32 [131072], P('row'), may hold values from 0 to 1
- objective: float32 [131072], P('col'), may hold values from -68 to 68
- lower_bound: float32 [131072], P('col'), may hold values from -1.5 to 1.5
- upper_bound: float32 [131072], P('col'), may hold values from -1.5 to 1.5
- variable_kind: int32 [131072], P('col'), may hold values from 0 to 3
Outputs:
- primal_residual: float32 [2, 131072], P(None, ('row', 'col'))
- dual_residual: float32 [2, 131072], P(None, ('col', 'row'))
- metrics: float32 [2, 3], replicated
The draws below stay inside these ranges and needn't reach their ends.
Inputs may be any that keep to these rules, and one draw needn't show every extreme that they name: `tile_counts`: slots below the count of a list hold live tiles, the others are padding; some list has all 16 slots live. `tile_rows`: in each constraint group, the first (8) slots of its lists name every block row of the group exactly once; later slots name any block row, and repeated tiles add. `tile_columns`: in each variable group, the first (8) slots of its lists name every block column of the group exactly once; later slots name any block column, and repeated tiles add. `constraint_kind`: 0 marks an equality, 1 a constraint of the form at least. `variable_kind`: 0 free, 1 lower bound only, 2 upper bound only, 3 both bounds.
All inputs are finite; a program needn't handle non-finite values.
Results may differ from the reference program's by a relative error of at most 0.0003.
Values sent between devices are 32-bit elements; how exact they have to be, the bound alone decides.
No kernel may reach another device: no remote copies, remote signals or barrier semaphores. Data moves between devices by JAX's collectives and lax.ppermute only.
A program may use at most 64 MiB of HBM per device.

```python
import math
import jax
import jax.numpy as jnp
from jax import lax

BLK = 512
TILES_DEV = 16
CANDS = 2
RBG = 64
CBG = 32
NROW = 131072
NCOL = 131072
N_ROW = 4
N_COL = 8


def rising_vector(key, length):
    first_key, second_key = jax.random.split(key)
    position = jnp.arange(length, dtype=jnp.float32) / length
    values = jnp.clip(jax.random.normal(first_key, (length,), jnp.float32), -5.0, 5.0)
    growth = jnp.exp(position * math.log(3.0))
    spread = jnp.exp(jax.random.uniform(second_key, (length,), jnp.float32, 0.0, math.log(10.0)))
    return (0.15 * values * spread * growth).astype(jnp.float32)


def draw_requirement(key, part):
    return rising_vector(jax.random.fold_in(key, 11), NROW)


def draw_objective(key, part):
    return rising_vector(jax.random.fold_in(key, 12), NCOL)


def draw_tile_counts(key, part):
    first_key, second_key = jax.random.split(jax.random.fold_in(key, 13))
    counts = jax.random.randint(first_key, (N_ROW * N_COL,), TILES_DEV // 2, TILES_DEV + 1)
    chosen = jax.random.randint(second_key, (), 0, N_ROW * N_COL)
    flattened = jnp.where(jnp.arange(N_ROW * N_COL) == chosen, TILES_DEV, counts)
    return flattened.reshape(N_ROW, N_COL).astype(jnp.int32)


def draw_tile_rows(key, part):
    half = TILES_DEV // 2
    perm_keys = jax.random.split(jax.random.fold_in(key, 21), N_ROW)
    covering = jax.vmap(lambda single: jax.random.permutation(single, RBG))(perm_keys)
    covering = covering.reshape(N_ROW, N_COL, half)
    extra = jax.random.randint(jax.random.fold_in(key, 22), (N_ROW, N_COL, TILES_DEV - half), 0, RBG)
    return jnp.concatenate([covering.astype(jnp.int32), extra.astype(jnp.int32)], axis=2)


def draw_tile_columns(key, part):
    half = TILES_DEV // 2
    perm_keys = jax.random.split(jax.random.fold_in(key, 31), N_COL)
    covering = jax.vmap(lambda single: jax.random.permutation(single, CBG))(perm_keys)
    covering = jnp.transpose(covering.reshape(N_COL, N_ROW, half), (1, 0, 2))
    extra = jax.random.randint(jax.random.fold_in(key, 32), (N_ROW, N_COL, TILES_DEV - half), 0, CBG)
    return jnp.concatenate([covering.astype(jnp.int32), extra.astype(jnp.int32)], axis=2)


def touch_ends(entries, rng, smallest, high):
    longest = entries.shape.index(max(entries.shape))
    spots = []
    for shift in (0, 1):
        where = [jax.random.randint(jax.random.fold_in(rng, axis), (), 0, length) for axis, length in enumerate(entries.shape)]
        where[longest] = (where[longest] + shift) % entries.shape[longest]
        spots.append(tuple(where))
    return entries.at[spots[0]].set(smallest).at[spots[1]].set(high)


def level_of(own_key, extent, cuts, low, largest):
    def one(dim, parts):
        heights = jax.random.uniform(jax.random.fold_in(jax.random.fold_in(own_key, 6), dim), (parts,), jnp.float32, low / len(cuts), largest / len(cuts))
        return jnp.repeat(jnp.exp(heights), extent[dim] // parts).reshape((-1,) + (1,) * (len(extent) - dim - 1))

    gain = one(*cuts[0])
    for cut in cuts[1:]:
        gain = gain * one(*cut)
    return gain


def gaussian(stream_key, shape, scale, limit, shards=(), kind=jnp.bfloat16):
    factor_of = level_of(stream_key, shape, shards, -0.22, 0.18) if shards else 1.0
    entries = jax.random.normal(stream_key, shape, jnp.float32) * scale * factor_of
    return jnp.minimum(jnp.maximum(entries, -limit), limit).astype(kind)


def setup_inputs(seed: int = 0) -> dict:
    keys = jax.random.split(jax.random.key(seed), 13)
    return {
        "matrix_tiles": gaussian(keys[0], (N_ROW, N_COL, TILES_DEV, BLK, BLK), BLK ** -0.5, 0.25, ((0, 4), (1, 8)), jnp.float32),
        "tile_rows": draw_tile_rows(jax.random.fold_in(keys[12], 71), 0),
        "tile_columns": draw_tile_columns(jax.random.fold_in(keys[12], 71), 0),
        "tile_counts": draw_tile_counts(jax.random.fold_in(keys[12], 71), 0),
        "primal_iter": gaussian(keys[4], (CANDS, NCOL), 1.0, 6.0, ((1, 32),), jnp.float32),
        "dual_iter": gaussian(keys[5], (CANDS, NROW), 1.0, 6.0, ((1, 32),), jnp.float32),
        "requirement": draw_requirement(jax.random.fold_in(keys[12], 71), 0),
        "constraint_kind": touch_ends(jax.random.randint(keys[7], (NROW,), 0, 2), jax.random.fold_in(keys[7], 1), 0, 1).astype(jnp.int32),
        "objective": draw_objective(jax.random.fold_in(keys[12], 71), 0),
        "lower_bound": jnp.clip(jax.random.uniform(keys[9], (NCOL,), jnp.float32, -1.5, 1.5) * level_of(keys[9], (NCOL,), ((0, 8),), -0.4, 0.0), -1.5, 1.5),
        "upper_bound": jnp.clip(jax.random.uniform(keys[10], (NCOL,), jnp.float32, -1.5, 1.5) * level_of(keys[10], (NCOL,), ((0, 8),), -0.4, 0.0), -1.5, 1.5),
        "variable_kind": touch_ends(jax.random.randint(keys[11], (NCOL,), 0, 4), jax.random.fold_in(keys[11], 1), 0, 3).astype(jnp.int32),
    }


HIGHEST_PRECISION = lax.Precision.HIGHEST

def primal_side(product, require_part, kind_part, dual_part):
    difference = require_part[None, :] - product
    residual = jnp.where(kind_part[None, :] == 1, jnp.maximum(difference, 0.0), difference)
    return (residual, lax.optimization_barrier(jnp.sum(residual * residual, axis=1)), jnp.sum(require_part * require_part), lax.optimization_barrier(jnp.sum(require_part[None, :] * dual_part, axis=1)))

def dual_side(transposed, objective, lower_bound, upper_bound, variable_kind, primal_part):
    reduced = objective[None, :] - transposed
    lower_active = (variable_kind == 1) | (variable_kind == 3)
    upper_active = (variable_kind == 2) | (variable_kind == 3)
    multiplier = jnp.where(lower_active[None, :], jnp.maximum(reduced, 0.0), 0.0) + jnp.where(upper_active[None, :], jnp.minimum(reduced, 0.0), 0.0)
    residual = reduced - multiplier
    bound_sum = lax.optimization_barrier(jnp.sum(lower_bound[None, :] * jnp.maximum(multiplier, 0.0) + upper_bound[None, :] * jnp.minimum(multiplier, 0.0), axis=1))
    return (residual, lax.optimization_barrier(jnp.sum(residual * residual, axis=1)), jnp.sum(objective * objective), lax.optimization_barrier(jnp.sum(objective[None, :] * primal_part, axis=1)), bound_sum)

def finish(primal_square, require_square, require_dot, dual_square, objective_square, objective_dot, bound_sum):
    primal_ratio = jnp.sqrt(primal_square) / (1.0 + jnp.sqrt(require_square))
    dual_ratio = jnp.sqrt(dual_square) / (1.0 + jnp.sqrt(objective_square))
    dual_value = require_dot + bound_sum
    duality_gap = jnp.abs(objective_dot - dual_value) / (1.0 + jnp.abs(objective_dot) + jnp.abs(dual_value))
    return jnp.stack([primal_ratio, dual_ratio, duality_gap], axis=1)

def reference(matrix_tiles, tile_rows, tile_columns, tile_counts, primal_iter, dual_iter, requirement, constraint_kind, objective, lower_bound, upper_bound, variable_kind):
    block_size = matrix_tiles.shape[-1]
    slot_count = matrix_tiles.shape[2]
    groups = N_ROW * N_COL
    row_blocks = requirement.shape[0] // block_size // N_ROW
    column_blocks = objective.shape[0] // block_size // N_COL
    candidates = primal_iter.shape[0]
    primal_blocks = primal_iter.reshape(candidates, -1, block_size)
    dual_blocks = dual_iter.reshape(candidates, -1, block_size)
    flat_tiles = matrix_tiles.reshape(groups, slot_count, block_size, block_size)

    def accumulate(totals, inputs):
        product, transposed = totals
        own_tiles, rows_here, columns_here, count_here, device_index = inputs
        global_rows = device_index // N_COL * row_blocks + rows_here
        global_columns = device_index % N_COL * column_blocks + columns_here
        active = (lax.iota(jnp.int32, slot_count) < count_here).astype(own_tiles.dtype)
        primal_pick = primal_blocks[:, global_columns, :] * active[None, :, None]
        dual_pick = dual_blocks[:, global_rows, :] * active[None, :, None]
        tile_product = jnp.einsum('tij,stj->sti', own_tiles, primal_pick, precision=HIGHEST_PRECISION)
        tile_transposed = jnp.einsum('tij,sti->stj', own_tiles, dual_pick, precision=HIGHEST_PRECISION)
        product = product.at[:, global_rows, :].add(tile_product)
        transposed = transposed.at[:, global_columns, :].add(tile_transposed)
        return ((product, transposed), None)
    start = (jnp.zeros(dual_blocks.shape, matrix_tiles.dtype), jnp.zeros(primal_blocks.shape, matrix_tiles.dtype))
    inputs = (flat_tiles, tile_rows.reshape(groups, slot_count), tile_columns.reshape(groups, slot_count), tile_counts.reshape(groups), jnp.arange(groups, dtype=jnp.int32))
    (product, transposed), _ = lax.scan(accumulate, start, inputs)
    product = product.reshape(candidates, -1)
    transposed = transposed.reshape(candidates, -1)
    primal_residual, primal_square, require_square, require_dot = primal_side(product, requirement, constraint_kind, dual_iter)
    dual_residual, dual_square, objective_square, objective_dot, bound_sum = dual_side(transposed, objective, lower_bound, upper_bound, variable_kind, primal_iter)
    metrics = finish(primal_square, require_square, require_dot, dual_square, objective_square, objective_dot, bound_sum)
    return (primal_residual, dual_residual, metrics)
```

```python
import functools

import jax
import jax.numpy as jnp
from jax import lax
from jax.experimental import pallas as pl
from jax.experimental.pallas import tpu as pltpu
from jax.sharding import PartitionSpec as P

LANES = 128
SUB = 8
F32 = jnp.float32


def bits_of(count):
    return count.bit_length() - 1


def swap(value, axis, bit, count):
    return lax.ppermute(value, axis, [(i, i ^ bit) for i in range(count)])


def flip_bits(index, bits):
    out = jnp.int32(0)
    for bit in range(bits):
        out = out | (((index >> bit) & 1) << (bits - 1 - bit))
    return out


def tile_kernel(
    rows_ref,
    columns_ref,
    count_ref,
    primal_ref,
    dual_ref,
    tiles_ref,
    *refs,
    slot_count,
    block_size,
    row_devices,
    col_devices,
    row_share,
    column_share,
    extra_axes,
):
    extras = len(extra_axes)
    extra_in = refs[:extras]
    product_keep, product_send, transposed_keep, transposed_send = refs[extras : extras + 4]
    extra_out = refs[extras + 4 : 2 * extras + 4]
    tiles, product, transposed, tile_sems, extra_sems = refs[2 * extras + 4 :]
    my_row = lax.axis_index("row")
    my_col = lax.axis_index("col")
    live = count_ref[0, 0]

    def tile_copy(slot):
        return pltpu.make_async_copy(
            tiles_ref.at[0, 0, slot], tiles.at[slot], tile_sems.at[slot]
        )

    for slot in range(slot_count):

        @pl.when(slot < live)
        def _():
            tile_copy(slot).start()

    extra_copies = []
    for number, axis in enumerate(extra_axes):
        height = extra_out[number].shape[0]
        place = my_col if axis == "col" else my_row
        start = pl.multiple_of(place * height, SUB)
        extra_copies.append(
            pltpu.make_async_copy(
                extra_in[number].at[pl.ds(start, height)],
                extra_out[number],
                extra_sems.at[number],
            )
        )
        extra_copies[-1].start()

    product[...] = jnp.zeros(product.shape, F32)
    transposed[...] = jnp.zeros(transposed.shape, F32)
    chunks = block_size // LANES
    candidates = primal_ref.shape[1]
    row_blocks = row_share // block_size
    column_blocks = column_share // block_size

    def one_tile(slot, carry):
        tile_copy(slot).wait()
        block_row = rows_ref[0, 0, slot]
        block_column = columns_ref[0, 0, slot]
        row_owner = (block_row // row_blocks) ^ my_col
        column_owner = (block_column // column_blocks) ^ my_row
        row_inner = block_row % row_blocks
        column_inner = block_column % column_blocks
        primal = primal_ref[
            column_owner, :, pl.ds(pl.multiple_of(column_inner * block_size, LANES), block_size)
        ]
        dual = dual_ref[
            row_owner, :, pl.ds(pl.multiple_of(row_inner * block_size, LANES), block_size)
        ]
        spread = [
            [
                jnp.broadcast_to(primal[s : s + 1, k * LANES : (k + 1) * LANES], (SUB, LANES))
                for k in range(chunks)
            ]
            for s in range(candidates)
        ]
        dual_rows = jnp.concatenate([dual, jnp.zeros((SUB - candidates, block_size), F32)], 0)
        sums = [[jnp.zeros((SUB, LANES), F32) for _ in range(chunks)] for _ in range(candidates)]
        row_place = flip_bits(row_owner, bits_of(col_devices))
        column_place = flip_bits(column_owner, bits_of(row_devices))
        for band in range(chunks):
            dual_column = dual_rows[:, band * LANES : (band + 1) * LANES].T
            partial = [[] for _ in range(candidates)]
            for group in range(LANES // SUB):
                first = band * LANES + group * SUB
                part = [
                    tiles[slot, first : first + SUB, k * LANES : (k + 1) * LANES]
                    for k in range(chunks)
                ]
                for s in range(candidates):
                    weight = jnp.broadcast_to(
                        dual_column[group * SUB : (group + 1) * SUB, s : s + 1], (SUB, LANES)
                    )
                    total = part[0] * spread[s][0]
                    for k in range(1, chunks):
                        total = total + part[k] * spread[s][k]
                    partial[s].append(total)
                    for k in range(chunks):
                        sums[s][k] = sums[s][k] + part[k] * weight
            for s in range(candidates):
                turned = jnp.concatenate(partial[s], 0).T
                values = jnp.sum(turned, axis=0, keepdims=True)
                where = pl.ds(row_inner * chunks + band, 1)
                product[row_place, s, where, :] = product[row_place, s, where, :] + values
        for s in range(candidates):
            for k in range(chunks):
                values = jnp.sum(sums[s][k], axis=0, keepdims=True)
                where = pl.ds(column_inner * chunks + k, 1)
                transposed[column_place, s, where, :] = (
                    transposed[column_place, s, where, :] + values
                )
        return carry

    lax.fori_loop(0, live, one_tile, 0)
    half = col_devices // 2
    product_keep[...] = product[:half]
    product_send[...] = product[half:]
    half = row_devices // 2
    transposed_keep[...] = transposed[:half]
    transposed_send[...] = transposed[half:]
    for copy in extra_copies:
        copy.wait()


def side_kernel(
    product_keep,
    product_got,
    transposed_keep,
    transposed_got,
    require_ref,
    row_kind_ref,
    objective_ref,
    lower_ref,
    upper_ref,
    column_kind_ref,
    primal_ref,
    dual_ref,
    primal_out,
    dual_out,
    stats_out,
):
    candidates = primal_ref.shape[0]
    require = require_ref[...]
    row_kind = row_kind_ref[...]
    objective = objective_ref[...]
    lower = lower_ref[...]
    upper = upper_ref[...]
    column_kind = column_kind_ref[...]
    height = require.shape[0]
    width = objective.shape[0]

    def rows_of(ref, s, count):
        return jnp.concatenate(
            [ref[s : s + 1, k * LANES : (k + 1) * LANES] for k in range(count)], 0
        )

    def flat(value):
        return jnp.sum(value, axis=0, keepdims=True)

    lower_active = (column_kind == 1) | (column_kind == 3)
    upper_active = (column_kind == 2) | (column_kind == 3)
    stats = []
    for s in range(candidates):
        difference = require - (product_keep[0, s] + product_got[0, s])
        residual = jnp.where(row_kind == 1, jnp.maximum(difference, 0.0), difference)
        for k in range(height):
            primal_out[s : s + 1, k * LANES : (k + 1) * LANES] = residual[k : k + 1, :]
        reduced = objective - (transposed_keep[0, s] + transposed_got[0, s])
        multiplier = jnp.where(lower_active, jnp.maximum(reduced, 0.0), 0.0) + jnp.where(
            upper_active, jnp.minimum(reduced, 0.0), 0.0
        )
        dual_residual = reduced - multiplier
        for k in range(width):
            dual_out[s : s + 1, k * LANES : (k + 1) * LANES] = dual_residual[k : k + 1, :]
        stats += [
            flat(residual * residual),
            flat(dual_residual * dual_residual),
            flat(require * rows_of(dual_ref, s, height)),
            flat(objective * rows_of(primal_ref, s, width)),
            flat(lower * jnp.maximum(multiplier, 0.0) + upper * jnp.minimum(multiplier, 0.0)),
            flat(require * require),
            flat(objective * objective),
            jnp.zeros((1, LANES), F32),
        ]
    local = jnp.concatenate(stats, 0)
    for k in range(stats_out.shape[0]):
        stats_out[k] = local


def metric_kernel(stats_ref, out_ref):
    candidates = out_ref.shape[0]
    total = stats_ref[0]
    for k in range(1, stats_ref.shape[0]):
        total = total + stats_ref[k]
    total = jnp.broadcast_to(jnp.sum(total, axis=1, keepdims=True), total.shape)
    lines = []
    for s in range(candidates):
        line = [total[s * SUB + k : s * SUB + k + 1, :] for k in range(7)]
        primal_square, dual_square, require_dot, objective_dot, bound_sum = line[:5]
        require_square, objective_square = line[5:]
        dual_value = require_dot + bound_sum
        primal_ratio = jnp.sqrt(primal_square) / (1.0 + jnp.sqrt(require_square))
        dual_ratio = jnp.sqrt(dual_square) / (1.0 + jnp.sqrt(objective_square))
        gap = jnp.abs(objective_dot - dual_value) / (
            1.0 + jnp.abs(objective_dot) + jnp.abs(dual_value)
        )
        lane = lax.broadcasted_iota(jnp.int32, primal_ratio.shape, 1)
        lines.append(jnp.where(lane == 0, primal_ratio, jnp.where(lane == 1, dual_ratio, gap)))
    out_ref[...] = jnp.concatenate(lines, 0)[:, : out_ref.shape[1]]


def on_device(
    matrix_tiles,
    tile_rows,
    tile_columns,
    tile_counts,
    primal_iter,
    dual_iter,
    requirement,
    constraint_kind,
    objective,
    lower_bound,
    upper_bound,
    variable_kind,
    *,
    row_devices,
    col_devices,
):
    slot_count = matrix_tiles.shape[2]
    block_size = matrix_tiles.shape[-1]
    candidates, row_share = dual_iter.shape
    column_share = primal_iter.shape[1]
    primal_group = primal_iter[None]
    dual_group = dual_iter[None]
    for step in range(max(bits_of(row_devices), bits_of(col_devices))):
        bit = 1 << step
        primal_got = swap(primal_group, "row", bit, row_devices) if bit < row_devices else None
        dual_got = swap(dual_group, "col", bit, col_devices) if bit < col_devices else None
        if primal_got is not None:
            primal_group = jnp.concatenate([primal_group, primal_got], 0)
        if dual_got is not None:
            dual_group = jnp.concatenate([dual_group, dual_got], 0)

    extras = (
        (requirement, "col", row_share),
        (constraint_kind, "col", row_share),
        (objective, "row", column_share),
        (lower_bound, "row", column_share),
        (upper_bound, "row", column_share),
        (variable_kind, "row", column_share),
    )
    smem = pl.BlockSpec(memory_space=pltpu.SMEM)
    vmem = pl.BlockSpec(memory_space=pltpu.VMEM)
    hbm = pl.BlockSpec(memory_space=pl.ANY)
    row_height = row_share // LANES
    column_height = column_share // LANES
    product_shape = (col_devices, candidates, row_height, LANES)
    transposed_shape = (row_devices, candidates, column_height, LANES)

    def half_of(shape):
        return jax.ShapeDtypeStruct((shape[0] // 2,) + shape[1:], F32)

    outs = pl.pallas_call(
        functools.partial(
            tile_kernel,
            slot_count=slot_count,
            block_size=block_size,
            row_devices=row_devices,
            col_devices=col_devices,
            row_share=row_share,
            column_share=column_share,
            extra_axes=tuple(axis for _, axis, _ in extras),
        ),
        name="tile_pass",
        in_specs=[smem, smem, smem, vmem, vmem, hbm] + [hbm] * len(extras),
        out_specs=[vmem] * (4 + len(extras)),
        out_shape=[half_of(product_shape)] * 2
        + [half_of(transposed_shape)] * 2
        + [
            jax.ShapeDtypeStruct((share // LANES, LANES), value.dtype)
            for value, _, share in extras
        ],
        scratch_shapes=[
            pltpu.VMEM((slot_count, block_size, block_size), F32),
            pltpu.VMEM(product_shape, F32),
            pltpu.VMEM(transposed_shape, F32),
            pltpu.SemaphoreType.DMA((slot_count,)),
            pltpu.SemaphoreType.DMA((len(extras),)),
        ],
        compiler_params=pltpu.CompilerParams(vmem_limit_bytes=32 << 20),
    )(
        tile_rows,
        tile_columns,
        tile_counts,
        primal_group,
        dual_group,
        matrix_tiles,
        *[value.reshape(-1, LANES) for value, _, _ in extras],
    )
    product_keep, product_send, transposed_keep, transposed_send = outs[:4]
    for step in range(max(bits_of(row_devices), bits_of(col_devices))):
        bit = 1 << step
        product_got = swap(product_send, "col", bit, col_devices) if bit < col_devices else None
        transposed_got = (
            swap(transposed_send, "row", bit, row_devices) if bit < row_devices else None
        )
        if bit < col_devices:
            half = product_keep.shape[0] // 2
            if half:
                product_send = product_keep[half:] + product_got[half:]
                product_keep = product_keep[:half] + product_got[:half]
            else:
                product_last = product_got
        if bit < row_devices:
            half = transposed_keep.shape[0] // 2
            if half:
                transposed_send = transposed_keep[half:] + transposed_got[half:]
                transposed_keep = transposed_keep[:half] + transposed_got[:half]
            else:
                transposed_last = transposed_got

    devices = row_devices * col_devices
    stats_rows = candidates * SUB
    primal_residual, dual_residual, stats = pl.pallas_call(
        side_kernel,
        name="sides",
        in_specs=[vmem] * 12,
        out_specs=[vmem] * 3,
        out_shape=[
            jax.ShapeDtypeStruct(dual_iter.shape, F32),
            jax.ShapeDtypeStruct(primal_iter.shape, F32),
            jax.ShapeDtypeStruct((devices, stats_rows, LANES), F32),
        ],
    )(
        product_keep,
        product_last,
        transposed_keep,
        transposed_last,
        *outs[4:],
        primal_iter,
        dual_iter,
    )
    shared = lax.all_to_all(stats, ("row", "col"), 0, 0)
    metrics = pl.pallas_call(
        metric_kernel,
        name="metrics",
        in_specs=[vmem],
        out_specs=vmem,
        out_shape=jax.ShapeDtypeStruct((candidates, 3), F32),
    )(shared)
    return (primal_residual, dual_residual, metrics)


def solution(mesh):
    placed = (
        P("row", "col", None, None, None),
        P("row", "col", None),
        P("row", "col", None),
        P("row", "col"),
        P(None, ("col", "row")),
        P(None, ("row", "col")),
        P("row"),
        P("row"),
        P("col"),
        P("col"),
        P("col"),
        P("col"),
    )
    return jax.shard_map(
        functools.partial(
            on_device, row_devices=mesh.shape["row"], col_devices=mesh.shape["col"]
        ),
        mesh=mesh,
        in_specs=placed,
        out_specs=(P(None, ("row", "col")), P(None, ("col", "row")), P()),
        check_vma=False,
    )
```

```python
import functools

import jax
import jax.numpy as jnp
from jax import lax
from jax.experimental import pallas as pl
from jax.experimental.pallas import tpu as pltpu
from jax.sharding import PartitionSpec as P

LANES = 128
SUB = 8
F32 = jnp.float32


def bits_of(count):
    return count.bit_length() - 1


def swap(value, axis, bit, count):
    return lax.ppermute(value, axis, [(i, i ^ bit) for i in range(count)])


def in_hbm(value):
    return pltpu.with_memory_space_constraint(value, pltpu.HBM)


def crossed(count):
    return [bit | 1 for bit in plain(count)]


def plain(count):
    return [1 << step for step in range(bits_of(count))]


def place_of(index, bits, cross):
    low = index & 1
    if cross:
        for bit in range(1, bits):
            low = low ^ ((index >> bit) & 1)
    out = low << (bits - 1)
    for bit in range(1, bits):
        out = out | (((index >> bit) & 1) << (bits - 1 - bit))
    return out


def tile_kernel(
    rows_ref,
    columns_ref,
    count_ref,
    tiles_ref,
    *refs,
    slot_count,
    block_size,
    row_devices,
    col_devices,
    row_share,
    column_share,
    extra_axes,
):
    extras = len(extra_axes)
    primal_pieces, refs = refs[:row_devices], refs[row_devices:]
    dual_pieces, refs = refs[:col_devices], refs[col_devices:]
    extra_in, refs = refs[:extras], refs[extras:]
    product_keep, product_send, transposed_keep, transposed_send = refs[:4]
    extra_out, refs = refs[4 : extras + 4], refs[extras + 4 :]
    tiles, primal_ref, dual_ref, product, transposed, tile_sems, extra_sems = refs
    my_row = lax.axis_index("row")
    my_col = lax.axis_index("col")
    live = count_ref[0, 0]

    def tile_copy(slot):
        return pltpu.make_async_copy(
            tiles_ref.at[0, 0, slot], tiles.at[slot], tile_sems.at[slot]
        )

    for slot in range(slot_count):

        @pl.when(slot < live)
        def _():
            tile_copy(slot).start()

    extra_copies = []
    for number, axis in enumerate(extra_axes):
        height = extra_out[number].shape[0]
        place = my_col if axis == "col" else my_row
        start = pl.multiple_of(place * height, SUB)
        extra_copies.append(
            pltpu.make_async_copy(
                extra_in[number].at[pl.ds(start, height)],
                extra_out[number],
                extra_sems.at[number],
            )
        )
        extra_copies[-1].start()

    for number, piece in enumerate(primal_pieces):
        primal_ref[number] = piece[...]
    for number, piece in enumerate(dual_pieces):
        dual_ref[number] = piece[...]
    product[...] = jnp.zeros(product.shape, F32)
    transposed[...] = jnp.zeros(transposed.shape, F32)
    chunks = block_size // LANES
    candidates = primal_ref.shape[1]
    row_blocks = row_share // block_size
    column_blocks = column_share // block_size

    def one_tile(slot, carry):
        tile_copy(slot).wait()
        block_row = rows_ref[0, 0, slot]
        block_column = columns_ref[0, 0, slot]
        row_owner = (block_row // row_blocks) ^ my_col
        column_owner = (block_column // column_blocks) ^ my_row
        row_inner = block_row % row_blocks
        column_inner = block_column % column_blocks
        primal = primal_ref[
            column_owner, :, pl.ds(pl.multiple_of(column_inner * block_size, LANES), block_size)
        ]
        dual = dual_ref[
            row_owner, :, pl.ds(pl.multiple_of(row_inner * block_size, LANES), block_size)
        ]
        spread = [
            [
                jnp.broadcast_to(primal[s : s + 1, k * LANES : (k + 1) * LANES], (SUB, LANES))
                for k in range(chunks)
            ]
            for s in range(candidates)
        ]
        dual_rows = jnp.concatenate([dual, jnp.zeros((SUB - candidates, block_size), F32)], 0)
        sums = [[jnp.zeros((SUB, LANES), F32) for _ in range(chunks)] for _ in range(candidates)]
        row_place = place_of(row_owner, bits_of(col_devices), True)
        column_place = place_of(column_owner, bits_of(row_devices), False)
        for band in range(chunks):
            dual_column = dual_rows[:, band * LANES : (band + 1) * LANES].T
            partial = [[] for _ in range(candidates)]
            for group in range(LANES // SUB):
                first = band * LANES + group * SUB
                part = [
                    tiles[slot, first : first + SUB, k * LANES : (k + 1) * LANES]
                    for k in range(chunks)
                ]
                for s in range(candidates):
                    weight = jnp.broadcast_to(
                        dual_column[group * SUB : (group + 1) * SUB, s : s + 1], (SUB, LANES)
                    )
                    total = part[0] * spread[s][0]
                    for k in range(1, chunks):
                        total = total + part[k] * spread[s][k]
                    partial[s].append(total)
                    for k in range(chunks):
                        sums[s][k] = sums[s][k] + part[k] * weight
            for s in range(candidates):
                turned = jnp.concatenate(partial[s], 0).T
                values = jnp.sum(turned, axis=0, keepdims=True)
                where = pl.ds(row_inner * chunks + band, 1)
                product[row_place, s, where, :] = product[row_place, s, where, :] + values
        for s in range(candidates):
            for k in range(chunks):
                values = jnp.sum(sums[s][k], axis=0, keepdims=True)
                where = pl.ds(column_inner * chunks + k, 1)
                transposed[column_place, s, where, :] = (
                    transposed[column_place, s, where, :] + values
                )
        return carry

    lax.fori_loop(0, live, one_tile, 0)
    half = col_devices // 2
    product_keep[...] = product[:half]
    product_send[...] = product[half:]
    half = row_devices // 2
    transposed_keep[...] = transposed[:half]
    transposed_send[...] = transposed[half:]
    for copy in extra_copies:
        copy.wait()


def side_kernel(
    product_keep,
    product_got,
    transposed_keep,
    transposed_got,
    require_ref,
    row_kind_ref,
    objective_ref,
    lower_ref,
    upper_ref,
    column_kind_ref,
    primal_ref,
    dual_ref,
    primal_out,
    dual_out,
    stats_out,
):
    candidates = primal_ref.shape[0]
    require = require_ref[...]
    row_kind = row_kind_ref[...]
    objective = objective_ref[...]
    lower = lower_ref[...]
    upper = upper_ref[...]
    column_kind = column_kind_ref[...]
    height = require.shape[0]
    width = objective.shape[0]

    def rows_of(ref, s, count):
        return jnp.concatenate(
            [ref[s : s + 1, k * LANES : (k + 1) * LANES] for k in range(count)], 0
        )

    def flat(value):
        return jnp.sum(value, axis=0, keepdims=True)

    lower_active = (column_kind == 1) | (column_kind == 3)
    upper_active = (column_kind == 2) | (column_kind == 3)
    stats = []
    for s in range(candidates):
        difference = require - (product_keep[0, s] + product_got[0, s])
        residual = jnp.where(row_kind == 1, jnp.maximum(difference, 0.0), difference)
        for k in range(height):
            primal_out[s : s + 1, k * LANES : (k + 1) * LANES] = residual[k : k + 1, :]
        reduced = objective - (transposed_keep[0, s] + transposed_got[0, s])
        multiplier = jnp.where(lower_active, jnp.maximum(reduced, 0.0), 0.0) + jnp.where(
            upper_active, jnp.minimum(reduced, 0.0), 0.0
        )
        dual_residual = reduced - multiplier
        for k in range(width):
            dual_out[s : s + 1, k * LANES : (k + 1) * LANES] = dual_residual[k : k + 1, :]
        stats += [
            flat(residual * residual),
            flat(dual_residual * dual_residual),
            flat(require * rows_of(dual_ref, s, height)),
            flat(objective * rows_of(primal_ref, s, width)),
            flat(lower * jnp.maximum(multiplier, 0.0) + upper * jnp.minimum(multiplier, 0.0)),
            flat(require * require),
            flat(objective * objective),
            jnp.zeros((1, LANES), F32),
        ]
    local = jnp.concatenate(stats, 0)
    local = jnp.broadcast_to(jnp.sum(local, axis=1, keepdims=True), local.shape)
    line = lax.broadcasted_iota(jnp.int32, local.shape, 0)
    lane = lax.broadcasted_iota(jnp.int32, local.shape, 1)
    packed = jnp.sum(jnp.where(line == lane, local, 0.0), axis=0, keepdims=True)
    stats_out[...] = jnp.broadcast_to(packed, stats_out.shape)


def metric_kernel(stats_ref, out_ref):
    candidates = out_ref.shape[0]
    total = jnp.sum(stats_ref[...], axis=0, keepdims=True)
    lines = []
    for s in range(candidates):
        line = [
            jnp.broadcast_to(total[:, s * SUB + k : s * SUB + k + 1], total.shape)
            for k in range(7)
        ]
        primal_square, dual_square, require_dot, objective_dot, bound_sum = line[:5]
        require_square, objective_square = line[5:]
        dual_value = require_dot + bound_sum
        primal_ratio = jnp.sqrt(primal_square) / (1.0 + jnp.sqrt(require_square))
        dual_ratio = jnp.sqrt(dual_square) / (1.0 + jnp.sqrt(objective_square))
        gap = jnp.abs(objective_dot - dual_value) / (
            1.0 + jnp.abs(objective_dot) + jnp.abs(dual_value)
        )
        lane = lax.broadcasted_iota(jnp.int32, primal_ratio.shape, 1)
        lines.append(jnp.where(lane == 0, primal_ratio, jnp.where(lane == 1, dual_ratio, gap)))
    out_ref[...] = jnp.concatenate(lines, 0)[:, : out_ref.shape[1]]


def on_device(
    matrix_tiles,
    tile_rows,
    tile_columns,
    tile_counts,
    primal_iter,
    dual_iter,
    requirement,
    constraint_kind,
    objective,
    lower_bound,
    upper_bound,
    variable_kind,
    *,
    row_devices,
    col_devices,
):
    slot_count = matrix_tiles.shape[2]
    block_size = matrix_tiles.shape[-1]
    candidates, row_share = dual_iter.shape
    column_share = primal_iter.shape[1]
    primal_pieces = {0: primal_iter}
    dual_pieces = {0: dual_iter}
    row_steps = plain(row_devices)
    col_steps = crossed(col_devices)
    for step in range(max(len(row_steps), len(col_steps))):
        if step < len(row_steps):
            bit = row_steps[step]
            primal_pieces.update(
                {
                    rel ^ bit: swap(value, "row", bit, row_devices)
                    for rel, value in primal_pieces.items()
                }
            )
        if step < len(col_steps):
            bit = (col_steps[1:] + col_steps[:1])[step]
            dual_pieces.update(
                {
                    rel ^ bit: swap(value, "col", bit, col_devices)
                    for rel, value in dual_pieces.items()
                }
            )

    extras = (
        (requirement, "col", row_share),
        (constraint_kind, "col", row_share),
        (objective, "row", column_share),
        (lower_bound, "row", column_share),
        (upper_bound, "row", column_share),
        (variable_kind, "row", column_share),
    )
    smem = pl.BlockSpec(memory_space=pltpu.SMEM)
    vmem = pl.BlockSpec(memory_space=pltpu.VMEM)
    hbm = pl.BlockSpec(memory_space=pltpu.HBM)
    row_height = row_share // LANES
    column_height = column_share // LANES
    product_shape = (col_devices, candidates, row_height, LANES)
    transposed_shape = (row_devices, candidates, column_height, LANES)

    def half_of(shape):
        return jax.ShapeDtypeStruct((shape[0] // 2,) + shape[1:], F32)

    outs = pl.pallas_call(
        functools.partial(
            tile_kernel,
            slot_count=slot_count,
            block_size=block_size,
            row_devices=row_devices,
            col_devices=col_devices,
            row_share=row_share,
            column_share=column_share,
            extra_axes=tuple(axis for _, axis, _ in extras),
        ),
        name="tile_pass",
        in_specs=[smem] * 3
        + [hbm]
        + [vmem] * (row_devices + col_devices)
        + [hbm] * len(extras),
        out_specs=[vmem] * (4 + len(extras)),
        out_shape=[half_of(product_shape)] * 2
        + [half_of(transposed_shape)] * 2
        + [
            jax.ShapeDtypeStruct((share // LANES, LANES), value.dtype)
            for value, _, share in extras
        ],
        scratch_shapes=[
            pltpu.VMEM((slot_count, block_size, block_size), F32),
            pltpu.VMEM((row_devices, candidates, column_share), F32),
            pltpu.VMEM((col_devices, candidates, row_share), F32),
            pltpu.VMEM(product_shape, F32),
            pltpu.VMEM(transposed_shape, F32),
            pltpu.SemaphoreType.DMA((slot_count,)),
            pltpu.SemaphoreType.DMA((len(extras),)),
        ],
        compiler_params=pltpu.CompilerParams(vmem_limit_bytes=32 << 20),
    )(
        in_hbm(tile_rows),
        in_hbm(tile_columns),
        tile_counts,
        in_hbm(matrix_tiles),
        in_hbm(primal_iter),
        *[primal_pieces[rel] for rel in range(1, row_devices)],
        in_hbm(dual_iter),
        *[dual_pieces[rel] for rel in range(1, col_devices)],
        *[in_hbm(value.reshape(-1, LANES)) for value, _, _ in extras],
    )
    product_keep, product_send, transposed_keep, transposed_send = outs[:4]
    for step in range(max(len(row_steps), len(col_steps))):
        if step < len(col_steps):
            product_got = swap(product_send, "col", col_steps[step], col_devices)
        if step < len(row_steps):
            transposed_got = swap(transposed_send, "row", row_steps[step], row_devices)
        if step + 1 < len(col_steps):
            half = product_keep.shape[0] // 2
            product_send = product_keep[half:] + product_got[half:]
            product_keep = product_keep[:half] + product_got[:half]
        if step + 1 < len(row_steps):
            half = transposed_keep.shape[0] // 2
            transposed_send = transposed_keep[half:] + transposed_got[half:]
            transposed_keep = transposed_keep[:half] + transposed_got[:half]

    devices = row_devices * col_devices
    primal_residual, dual_residual, stats = pl.pallas_call(
        side_kernel,
        name="sides",
        in_specs=[vmem] * 12,
        out_specs=[vmem] * 3,
        out_shape=[
            jax.ShapeDtypeStruct(dual_iter.shape, F32),
            jax.ShapeDtypeStruct(primal_iter.shape, F32),
            jax.ShapeDtypeStruct((devices, LANES), F32),
        ],
        compiler_params=pltpu.CompilerParams(vmem_limit_bytes=8 << 20),
    )(
        product_keep,
        product_got,
        transposed_keep,
        transposed_got,
        *outs[4:],
        primal_iter,
        dual_iter,
    )
    shared = lax.all_to_all(stats, ("row", "col"), 0, 0)
    metrics = pl.pallas_call(
        metric_kernel,
        name="metrics",
        in_specs=[vmem],
        out_specs=vmem,
        out_shape=jax.ShapeDtypeStruct((candidates, 3), F32),
        compiler_params=pltpu.CompilerParams(vmem_limit_bytes=8 << 20),
    )(shared)
    return (primal_residual, dual_residual, metrics)


def solution(mesh):
    placed = (
        P("row", "col", None, None, None),
        P("row", "col", None),
        P("row", "col", None),
        P("row", "col"),
        P(None, ("col", "row")),
        P(None, ("row", "col")),
        P("row"),
        P("row"),
        P("col"),
        P("col"),
        P("col"),
        P("col"),
    )
    return jax.shard_map(
        functools.partial(
            on_device, row_devices=mesh.shape["row"], col_devices=mesh.shape["col"]
        ),
        mesh=mesh,
        in_specs=placed,
        out_specs=(P(None, ("row", "col")), P(None, ("col", "row")), P()),
        check_vma=False,
    )
```

```python
import functools

import jax
import jax.numpy as jnp
from jax import lax
from jax.experimental import pallas as pl
from jax.experimental.pallas import tpu as pltpu
from jax.sharding import PartitionSpec as P

LANES = 128
SUB = 8
F32 = jnp.float32


def bits_of(count):
    return count.bit_length() - 1


def swap(value, axis, bit, count):
    return lax.ppermute(value, axis, [(i, i ^ bit) for i in range(count)])


def in_hbm(value):
    return pltpu.with_memory_space_constraint(value, pltpu.HBM)


def crossed(count):
    return [bit | 1 for bit in plain(count)]


def plain(count):
    return [1 << step for step in range(bits_of(count))]


def place_of(index, bits, cross):
    low = index & 1
    if cross:
        for bit in range(1, bits):
            low = low ^ ((index >> bit) & 1)
    out = low << (bits - 1)
    for bit in range(1, bits):
        out = out | (((index >> bit) & 1) << (bits - 1 - bit))
    return out


def tile_kernel(
    rows_ref,
    columns_ref,
    count_ref,
    tiles_ref,
    *refs,
    slot_count,
    block_size,
    row_devices,
    col_devices,
    row_share,
    column_share,
    extra_axes,
):
    extras = len(extra_axes)
    primal_pieces, refs = refs[:row_devices], refs[row_devices:]
    dual_pieces, refs = refs[:col_devices], refs[col_devices:]
    extra_in, refs = refs[:extras], refs[extras:]
    product_keep, product_send, transposed_keep, transposed_send = refs[:4]
    extra_out, refs = refs[4 : extras + 4], refs[extras + 4 :]
    tiles, primal_ref, dual_ref, product, transposed = refs[:5]
    dual_lines, dual_columns, partial, tile_sems, extra_sems = refs[5:]
    my_row = lax.axis_index("row")
    my_col = lax.axis_index("col")
    live = count_ref[0, 0]

    def tile_copy(slot):
        return pltpu.make_async_copy(
            tiles_ref.at[0, 0, slot], tiles.at[slot], tile_sems.at[slot]
        )

    for slot in range(slot_count):

        @pl.when(slot < live)
        def _():
            tile_copy(slot).start()

    extra_copies = []
    for number, axis in enumerate(extra_axes):
        height = extra_out[number].shape[0]
        place = my_col if axis == "col" else my_row
        start = pl.multiple_of(place * height, SUB)
        extra_copies.append(
            pltpu.make_async_copy(
                extra_in[number].at[pl.ds(start, height)],
                extra_out[number],
                extra_sems.at[number],
            )
        )
        extra_copies[-1].start()

    for number, piece in enumerate(primal_pieces):
        primal_ref[number] = piece[...]
    for number, piece in enumerate(dual_pieces):
        dual_ref[number] = piece[...]
    product[...] = jnp.zeros(product.shape, F32)
    transposed[...] = jnp.zeros(transposed.shape, F32)
    chunks = block_size // LANES
    candidates = primal_ref.shape[1]
    row_blocks = row_share // block_size
    column_blocks = column_share // block_size

    def row_of(slot):
        block_row = rows_ref[0, 0, slot]
        return (block_row // row_blocks) ^ my_col, block_row % row_blocks

    for slot in range(slot_count):
        owner, inner = row_of(slot)
        dual = dual_ref[owner, :, pl.ds(pl.multiple_of(inner * block_size, LANES), block_size)]
        dual_lines[slot * candidates : (slot + 1) * candidates, :] = dual
    for band in range(chunks):
        span = slice(band * LANES, (band + 1) * LANES)
        dual_columns[span, :] = dual_lines[:, span].T

    def multiply(slot, carry):
        tile_copy(slot).wait()
        folding = fold(jnp.maximum(slot - 1, 0), slot > 0)
        block_column = columns_ref[0, 0, slot]
        owner = (block_column // column_blocks) ^ my_row
        inner = block_column % column_blocks
        primal = primal_ref[owner, :, pl.ds(pl.multiple_of(inner * block_size, LANES), block_size)]
        spread = [
            [
                jnp.broadcast_to(primal[s : s + 1, k * LANES : (k + 1) * LANES], (SUB, LANES))
                for k in range(chunks)
            ]
            for s in range(candidates)
        ]
        lanes = [jnp.full((SUB, LANES), slot * candidates + s, jnp.int32) for s in range(candidates)]
        sums = [[jnp.zeros((SUB, LANES), F32) for _ in range(chunks)] for _ in range(candidates)]
        for first in range(0, block_size, SUB):
            if first % (block_size // 4) == 0:
                next(folding, None)
            part = [
                tiles[slot, first : first + SUB, k * LANES : (k + 1) * LANES]
                for k in range(chunks)
            ]
            column = dual_columns[first : first + SUB, :]
            for s in range(candidates):
                weight = jnp.take_along_axis(column, lanes[s], axis=1)
                total = part[0] * spread[s][0]
                for k in range(1, chunks):
                    total = total + part[k] * spread[s][k]
                partial[slot, s, first : first + SUB, :] = total
                for k in range(chunks):
                    sums[s][k] = sums[s][k] + part[k] * weight
        next(folding, None)
        place = place_of(owner, bits_of(row_devices), False)
        for s in range(candidates):
            for k in range(chunks):
                values = jnp.sum(sums[s][k], axis=0, keepdims=True)
                where = pl.ds(inner * chunks + k, 1)
                transposed[place, s, where, :] = transposed[place, s, where, :] + values
        return carry

    def fold(slot, valid):
        pieces = []
        half = block_size // 2
        for s in range(candidates):
            for first in range(0, block_size, half):
                whole = partial[slot, s, first : first + half, :]
                high = whole.astype(jnp.bfloat16)
                low = (whole - high.astype(F32)).astype(jnp.bfloat16)
                pieces.append(sum_lanes(high) + sum_lanes(low))
                yield
        owner, inner = row_of(slot)
        place = place_of(owner, bits_of(col_devices), True)
        for s in range(candidates):
            for band in range(chunks):
                first = band * LANES
                piece = pieces[s * 2 + first // half][:1, first % half : first % half + LANES]
                values = jnp.where(valid, piece, 0.0)
                where = pl.ds(inner * chunks + band, 1)
                product[place, s, where, :] = product[place, s, where, :] + values

    lax.fori_loop(0, live, multiply, 0)
    for _ in fold(jnp.maximum(live - 1, 0), live > 0):
        pass
    half = col_devices // 2
    product_keep[...] = product[:half]
    product_send[...] = product[half:]
    half = row_devices // 2
    transposed_keep[...] = transposed[:half]
    transposed_send[...] = transposed[half:]
    for copy in extra_copies:
        copy.wait()


def sum_lanes(value):
    ones = jnp.ones((SUB, value.shape[1]), value.dtype)
    return lax.dot_general(ones, value, (((1,), (1,)), ((), ())), preferred_element_type=F32)


def side_kernel(
    product_keep,
    product_got,
    transposed_keep,
    transposed_got,
    require_ref,
    row_kind_ref,
    objective_ref,
    lower_ref,
    upper_ref,
    column_kind_ref,
    primal_ref,
    dual_ref,
    primal_out,
    dual_out,
    stats_out,
):
    candidates = primal_ref.shape[0]
    require = require_ref[...]
    row_kind = row_kind_ref[...]
    objective = objective_ref[...]
    lower = lower_ref[...]
    upper = upper_ref[...]
    column_kind = column_kind_ref[...]
    height = require.shape[0]
    width = objective.shape[0]

    def rows_of(ref, s, count):
        return jnp.concatenate(
            [ref[s : s + 1, k * LANES : (k + 1) * LANES] for k in range(count)], 0
        )

    def flat(value):
        return jnp.sum(value, axis=0, keepdims=True)

    lower_active = (column_kind == 1) | (column_kind == 3)
    upper_active = (column_kind == 2) | (column_kind == 3)
    stats = []
    for s in range(candidates):
        difference = require - (product_keep[0, s] + product_got[0, s])
        residual = jnp.where(row_kind == 1, jnp.maximum(difference, 0.0), difference)
        for k in range(height):
            primal_out[s : s + 1, k * LANES : (k + 1) * LANES] = residual[k : k + 1, :]
        reduced = objective - (transposed_keep[0, s] + transposed_got[0, s])
        multiplier = jnp.where(lower_active, jnp.maximum(reduced, 0.0), 0.0) + jnp.where(
            upper_active, jnp.minimum(reduced, 0.0), 0.0
        )
        dual_residual = reduced - multiplier
        for k in range(width):
            dual_out[s : s + 1, k * LANES : (k + 1) * LANES] = dual_residual[k : k + 1, :]
        stats += [
            flat(residual * residual),
            flat(dual_residual * dual_residual),
            flat(require * rows_of(dual_ref, s, height)),
            flat(objective * rows_of(primal_ref, s, width)),
            flat(lower * jnp.maximum(multiplier, 0.0) + upper * jnp.minimum(multiplier, 0.0)),
            flat(require * require),
            flat(objective * objective),
            jnp.zeros((1, LANES), F32),
        ]
    local = jnp.concatenate(stats, 0)
    local = jnp.broadcast_to(jnp.sum(local, axis=1, keepdims=True), local.shape)
    line = lax.broadcasted_iota(jnp.int32, local.shape, 0)
    lane = lax.broadcasted_iota(jnp.int32, local.shape, 1)
    packed = jnp.sum(jnp.where(line == lane, local, 0.0), axis=0, keepdims=True)
    stats_out[...] = jnp.broadcast_to(packed, stats_out.shape)


def metric_kernel(stats_ref, out_ref):
    candidates = out_ref.shape[0]
    total = jnp.sum(stats_ref[...], axis=0, keepdims=True)
    lines = []
    for s in range(candidates):
        line = [
            jnp.broadcast_to(total[:, s * SUB + k : s * SUB + k + 1], total.shape)
            for k in range(7)
        ]
        primal_square, dual_square, require_dot, objective_dot, bound_sum = line[:5]
        require_square, objective_square = line[5:]
        dual_value = require_dot + bound_sum
        primal_ratio = jnp.sqrt(primal_square) / (1.0 + jnp.sqrt(require_square))
        dual_ratio = jnp.sqrt(dual_square) / (1.0 + jnp.sqrt(objective_square))
        gap = jnp.abs(objective_dot - dual_value) / (
            1.0 + jnp.abs(objective_dot) + jnp.abs(dual_value)
        )
        lane = lax.broadcasted_iota(jnp.int32, primal_ratio.shape, 1)
        lines.append(jnp.where(lane == 0, primal_ratio, jnp.where(lane == 1, dual_ratio, gap)))
    out_ref[...] = jnp.concatenate(lines, 0)[:, : out_ref.shape[1]]


def on_device(
    matrix_tiles,
    tile_rows,
    tile_columns,
    tile_counts,
    primal_iter,
    dual_iter,
    requirement,
    constraint_kind,
    objective,
    lower_bound,
    upper_bound,
    variable_kind,
    *,
    row_devices,
    col_devices,
):
    slot_count = matrix_tiles.shape[2]
    block_size = matrix_tiles.shape[-1]
    candidates, row_share = dual_iter.shape
    column_share = primal_iter.shape[1]
    primal_pieces = {0: primal_iter}
    dual_pieces = {0: dual_iter}
    row_steps = plain(row_devices)
    col_steps = crossed(col_devices)
    for step in range(max(len(row_steps), len(col_steps))):
        if step < len(row_steps):
            bit = row_steps[step]
            primal_pieces.update(
                {
                    rel ^ bit: swap(value, "row", bit, row_devices)
                    for rel, value in primal_pieces.items()
                }
            )
        if step < len(col_steps):
            bit = (col_steps[1:] + col_steps[:1])[step]
            dual_pieces.update(
                {
                    rel ^ bit: swap(value, "col", bit, col_devices)
                    for rel, value in dual_pieces.items()
                }
            )

    extras = (
        (requirement, "col", row_share),
        (constraint_kind, "col", row_share),
        (objective, "row", column_share),
        (lower_bound, "row", column_share),
        (upper_bound, "row", column_share),
        (variable_kind, "row", column_share),
    )
    smem = pl.BlockSpec(memory_space=pltpu.SMEM)
    vmem = pl.BlockSpec(memory_space=pltpu.VMEM)
    hbm = pl.BlockSpec(memory_space=pltpu.HBM)
    row_height = row_share // LANES
    column_height = column_share // LANES
    product_shape = (col_devices, candidates, row_height, LANES)
    transposed_shape = (row_devices, candidates, column_height, LANES)

    def half_of(shape):
        return jax.ShapeDtypeStruct((shape[0] // 2,) + shape[1:], F32)

    outs = pl.pallas_call(
        functools.partial(
            tile_kernel,
            slot_count=slot_count,
            block_size=block_size,
            row_devices=row_devices,
            col_devices=col_devices,
            row_share=row_share,
            column_share=column_share,
            extra_axes=tuple(axis for _, axis, _ in extras),
        ),
        name="tile_pass",
        in_specs=[smem] * 3
        + [hbm]
        + [vmem] * (row_devices + col_devices)
        + [hbm] * len(extras),
        out_specs=[vmem] * (4 + len(extras)),
        out_shape=[half_of(product_shape)] * 2
        + [half_of(transposed_shape)] * 2
        + [
            jax.ShapeDtypeStruct((share // LANES, LANES), value.dtype)
            for value, _, share in extras
        ],
        scratch_shapes=[
            pltpu.VMEM((slot_count, block_size, block_size), F32),
            pltpu.VMEM((row_devices, candidates, column_share), F32),
            pltpu.VMEM((col_devices, candidates, row_share), F32),
            pltpu.VMEM(product_shape, F32),
            pltpu.VMEM(transposed_shape, F32),
            pltpu.VMEM((LANES, block_size), F32),
            pltpu.VMEM((block_size, LANES), F32),
            pltpu.VMEM((slot_count, candidates, block_size, LANES), F32),
            pltpu.SemaphoreType.DMA((slot_count,)),
            pltpu.SemaphoreType.DMA((len(extras),)),
        ],
        compiler_params=pltpu.CompilerParams(vmem_limit_bytes=32 << 20),
    )(
        in_hbm(tile_rows),
        in_hbm(tile_columns),
        tile_counts,
        in_hbm(matrix_tiles),
        in_hbm(primal_iter),
        *[primal_pieces[rel] for rel in range(1, row_devices)],
        in_hbm(dual_iter),
        *[dual_pieces[rel] for rel in range(1, col_devices)],
        *[in_hbm(value.reshape(-1, LANES)) for value, _, _ in extras],
    )
    product_keep, product_send, transposed_keep, transposed_send = outs[:4]
    for step in range(max(len(row_steps), len(col_steps))):
        if step < len(col_steps):
            product_got = swap(product_send, "col", col_steps[step], col_devices)
        if step < len(row_steps):
            transposed_got = swap(transposed_send, "row", row_steps[step], row_devices)
        if step + 1 < len(col_steps):
            half = product_keep.shape[0] // 2
            product_send = product_keep[half:] + product_got[half:]
            product_keep = product_keep[:half] + product_got[:half]
        if step + 1 < len(row_steps):
            half = transposed_keep.shape[0] // 2
            transposed_send = transposed_keep[half:] + transposed_got[half:]
            transposed_keep = transposed_keep[:half] + transposed_got[:half]

    devices = row_devices * col_devices
    primal_residual, dual_residual, stats = pl.pallas_call(
        side_kernel,
        name="sides",
        in_specs=[vmem] * 12,
        out_specs=[vmem] * 3,
        out_shape=[
            jax.ShapeDtypeStruct(dual_iter.shape, F32),
            jax.ShapeDtypeStruct(primal_iter.shape, F32),
            jax.ShapeDtypeStruct((devices, LANES), F32),
        ],
        compiler_params=pltpu.CompilerParams(vmem_limit_bytes=8 << 20),
    )(
        product_keep,
        product_got,
        transposed_keep,
        transposed_got,
        *outs[4:],
        primal_iter,
        dual_iter,
    )
    shared = lax.all_to_all(stats, ("row", "col"), 0, 0)
    metrics = pl.pallas_call(
        metric_kernel,
        name="metrics",
        in_specs=[vmem],
        out_specs=vmem,
        out_shape=jax.ShapeDtypeStruct((candidates, 3), F32),
        compiler_params=pltpu.CompilerParams(vmem_limit_bytes=8 << 20),
    )(shared)
    return (primal_residual, dual_residual, metrics)


def solution(mesh):
    placed = (
        P("row", "col", None, None, None),
        P("row", "col", None),
        P("row", "col", None),
        P("row", "col"),
        P(None, ("col", "row")),
        P(None, ("row", "col")),
        P("row"),
        P("row"),
        P("col"),
        P("col"),
        P("col"),
        P("col"),
    )
    return jax.shard_map(
        functools.partial(
            on_device, row_devices=mesh.shape["row"], col_devices=mesh.shape["col"]
        ),
        mesh=mesh,
        in_specs=placed,
        out_specs=(P(None, ("row", "col")), P(None, ("col", "row")), P()),
        check_vma=False,
    )
```

```python
import functools

import jax
import jax.numpy as jnp
from jax import lax
from jax.experimental import pallas as pl
from jax.experimental.pallas import tpu as pltpu
from jax.sharding import PartitionSpec as P


LANES = 128
SUB = 8
EARLY = 3
F32 = jnp.float32


def bits_of(count):
    return count.bit_length() - 1


def swap(value, axis, bit, count):
    return lax.ppermute(value, axis, [(i, i ^ bit) for i in range(count)])


def in_hbm(value):
    return pltpu.with_memory_space_constraint(value, pltpu.HBM)


def crossed(count):
    return [bit | 1 for bit in plain(count)]


def plain(count):
    return [1 << step for step in range(bits_of(count))]


def place_of(index, bits, cross):
    low = index & 1
    if cross:
        for bit in range(1, bits):
            low = low ^ ((index >> bit) & 1)
    out = low << (bits - 1)
    for bit in range(1, bits):
        out = out | (((index >> bit) & 1) << (bits - 1 - bit))
    return out


def stage_kernel(primal_in, dual_in, primal_out, dual_out, sems):
    copies = [
        pltpu.make_async_copy(primal_in, primal_out, sems.at[0]),
        pltpu.make_async_copy(dual_in, dual_out, sems.at[1]),
    ]
    for copy in copies:
        copy.start()
    for copy in copies:
        copy.wait()


def early_kernel(tiles_ref, after_ref, out_ref, sems):
    copies = [
        pltpu.make_async_copy(tiles_ref.at[0, 0, slot], out_ref.at[slot], sems.at[slot])
        for slot in range(out_ref.shape[0])
    ]
    for copy in copies:
        copy.start()
    for copy in copies:
        copy.wait()


def gather_step(mine, value, axis, bit, count):
    got = swap(value, axis, bit, count)
    return jnp.concatenate([mine, got], 0)


def tile_kernel(
    rows_ref,
    columns_ref,
    count_ref,
    tiles_ref,
    *refs,
    slot_count,
    block_size,
    row_devices,
    col_devices,
    row_share,
    column_share,
    extra_axes,
    primal_order,
    dual_order,
):
    extras = len(extra_axes)
    (early_ref, primal_near, primal_far, dual_near, dual_far), refs = refs[:5], refs[5:]
    extra_in, refs = refs[:extras], refs[extras:]
    product_keep, product_send, transposed_keep, transposed_send = refs[:4]
    extra_out, refs = refs[4 : extras + 4], refs[extras + 4 :]
    tiles, primal_ref, dual_ref, product, transposed = refs[:5]
    dual_lines, dual_columns, partial, tile_sems, extra_sems = refs[5:]
    my_row = lax.axis_index("row")
    my_col = lax.axis_index("col")
    live = count_ref[0, 0]

    def tile_copy(slot):
        return pltpu.make_async_copy(
            tiles_ref.at[0, 0, slot],
            tiles.at[slot - early],
            tile_sems.at[slot - early],
        )

    early = early_ref.shape[0]
    for slot in range(early, slot_count):

        @pl.when(slot < live)
        def _():
            tile_copy(slot).start()

    extra_copies = []
    for number, axis in enumerate(extra_axes):
        height = extra_out[number].shape[0]
        place = my_col if axis == "col" else my_row
        start = pl.multiple_of(place * height, SUB)
        extra_copies.append(
            pltpu.make_async_copy(
                extra_in[number].at[pl.ds(start, height)],
                extra_out[number],
                extra_sems.at[number],
            )
        )
        extra_copies[-1].start()

    for number, rel in enumerate(primal_order):
        near = primal_near if number < primal_near.shape[0] else primal_far
        primal_ref[rel] = near[number % primal_near.shape[0]]
    for number, rel in enumerate(dual_order):
        near = dual_near if number < dual_near.shape[0] else dual_far
        dual_ref[rel] = near[number % dual_near.shape[0]]
    product[...] = jnp.zeros(product.shape, F32)
    transposed[...] = jnp.zeros(transposed.shape, F32)
    chunks = block_size // LANES
    candidates = primal_ref.shape[1]
    row_blocks = row_share // block_size
    column_blocks = column_share // block_size

    def row_of(slot):
        block_row = rows_ref[0, 0, slot]
        return (block_row // row_blocks) ^ my_col, block_row % row_blocks

    for slot in range(slot_count):
        owner, inner = row_of(slot)
        dual = dual_ref[owner, :, pl.ds(pl.multiple_of(inner * block_size, LANES), block_size)]
        dual_lines[slot * candidates : (slot + 1) * candidates, :] = dual
    for band in range(chunks):
        span = slice(band * LANES, (band + 1) * LANES)
        dual_columns[span, :] = dual_lines[:, span].T

    def multiply_early(slot, carry):
        multiply(slot, slot, early_ref)
        return carry

    def multiply_late(slot, carry):
        tile_copy(slot).wait()
        multiply(slot, slot - early, tiles)
        return carry

    def multiply(slot, place, source):
        folding = fold(jnp.maximum(slot - 1, 0), slot > 0)
        block_column = columns_ref[0, 0, slot]
        owner = (block_column // column_blocks) ^ my_row
        inner = block_column % column_blocks
        primal = primal_ref[owner, :, pl.ds(pl.multiple_of(inner * block_size, LANES), block_size)]
        spread = [
            [
                jnp.broadcast_to(primal[s : s + 1, k * LANES : (k + 1) * LANES], (SUB, LANES))
                for k in range(chunks)
            ]
            for s in range(candidates)
        ]
        lanes = [jnp.full((SUB, LANES), slot * candidates + s, jnp.int32) for s in range(candidates)]
        sums = [[jnp.zeros((SUB, LANES), F32) for _ in range(chunks)] for _ in range(candidates)]
        for first in range(0, block_size, SUB):
            if first % (block_size // 4) == 0:
                next(folding, None)
            part = [
                source[place, first : first + SUB, k * LANES : (k + 1) * LANES]
                for k in range(chunks)
            ]
            column = dual_columns[first : first + SUB, :]
            for s in range(candidates):
                weight = jnp.take_along_axis(column, lanes[s], axis=1)
                total = part[0] * spread[s][0]
                for k in range(1, chunks):
                    total = total + part[k] * spread[s][k]
                partial[slot, s, first : first + SUB, :] = total
                for k in range(chunks):
                    sums[s][k] = sums[s][k] + part[k] * weight
        next(folding, None)
        turn = place_of(owner, bits_of(row_devices), False)
        for s in range(candidates):
            for k in range(chunks):
                values = jnp.sum(sums[s][k], axis=0, keepdims=True)
                where = pl.ds(inner * chunks + k, 1)
                transposed[turn, s, where, :] = transposed[turn, s, where, :] + values

    def fold(slot, valid):
        pieces = []
        half = block_size // 2
        for s in range(candidates):
            for first in range(0, block_size, half):
                whole = partial[slot, s, first : first + half, :]
                high = whole.astype(jnp.bfloat16)
                low = (whole - high.astype(F32)).astype(jnp.bfloat16)
                pieces.append(sum_lanes(high) + sum_lanes(low))
                yield
        owner, inner = row_of(slot)
        place = place_of(owner, bits_of(col_devices), True)
        for s in range(candidates):
            for band in range(chunks):
                first = band * LANES
                piece = pieces[s * 2 + first // half][:1, first % half : first % half + LANES]
                values = jnp.where(valid, piece, 0.0)
                where = pl.ds(inner * chunks + band, 1)
                product[place, s, where, :] = product[place, s, where, :] + values

    lax.fori_loop(0, jnp.minimum(live, early), multiply_early, 0)
    lax.fori_loop(early, jnp.maximum(live, early), multiply_late, 0)
    for _ in fold(jnp.maximum(live - 1, 0), live > 0):
        pass
    half = col_devices // 2
    product_keep[...] = product[:half]
    product_send[...] = product[half:]
    half = row_devices // 2
    transposed_keep[...] = transposed[:half]
    transposed_send[...] = transposed[half:]
    for copy in extra_copies:
        copy.wait()


def sum_lanes(value):
    ones = jnp.ones((SUB, value.shape[1]), value.dtype)
    return lax.dot_general(ones, value, (((1,), (1,)), ((), ())), preferred_element_type=F32)


def side_kernel(
    product_keep,
    product_got,
    transposed_keep,
    transposed_got,
    require_ref,
    row_kind_ref,
    objective_ref,
    lower_ref,
    upper_ref,
    column_kind_ref,
    primal_ref,
    dual_ref,
    primal_out,
    dual_out,
    stats_out,
):
    candidates = primal_ref.shape[0]
    require = require_ref[...]
    row_kind = row_kind_ref[...]
    objective = objective_ref[...]
    lower = lower_ref[...]
    upper = upper_ref[...]
    column_kind = column_kind_ref[...]
    height = require.shape[0]
    width = objective.shape[0]

    def rows_of(ref, s, count):
        return jnp.concatenate(
            [ref[s : s + 1, k * LANES : (k + 1) * LANES] for k in range(count)], 0
        )

    def flat(value):
        return jnp.sum(value, axis=0, keepdims=True)

    lower_active = (column_kind == 1) | (column_kind == 3)
    upper_active = (column_kind == 2) | (column_kind == 3)
    stats = []
    for s in range(candidates):
        difference = require - (product_keep[0, s] + product_got[0, s])
        residual = jnp.where(row_kind == 1, jnp.maximum(difference, 0.0), difference)
        for k in range(height):
            primal_out[s : s + 1, k * LANES : (k + 1) * LANES] = residual[k : k + 1, :]
        reduced = objective - (transposed_keep[0, s] + transposed_got[0, s])
        multiplier = jnp.where(lower_active, jnp.maximum(reduced, 0.0), 0.0) + jnp.where(
            upper_active, jnp.minimum(reduced, 0.0), 0.0
        )
        dual_residual = reduced - multiplier
        for k in range(width):
            dual_out[s : s + 1, k * LANES : (k + 1) * LANES] = dual_residual[k : k + 1, :]
        stats += [
            flat(residual * residual),
            flat(dual_residual * dual_residual),
            flat(require * rows_of(dual_ref, s, height)),
            flat(objective * rows_of(primal_ref, s, width)),
            flat(lower * jnp.maximum(multiplier, 0.0) + upper * jnp.minimum(multiplier, 0.0)),
            flat(require * require),
            flat(objective * objective),
            jnp.zeros((1, LANES), F32),
        ]
    local = jnp.concatenate(stats, 0)
    local = jnp.broadcast_to(jnp.sum(local, axis=1, keepdims=True), local.shape)
    line = lax.broadcasted_iota(jnp.int32, local.shape, 0)
    lane = lax.broadcasted_iota(jnp.int32, local.shape, 1)
    packed = jnp.sum(jnp.where(line == lane, local, 0.0), axis=0, keepdims=True)
    stats_out[...] = jnp.broadcast_to(packed, stats_out.shape)


def metric_kernel(stats_ref, out_ref):
    candidates = out_ref.shape[0]
    total = jnp.sum(stats_ref[...], axis=0, keepdims=True)
    lines = []
    for s in range(candidates):
        line = [
            jnp.broadcast_to(total[:, s * SUB + k : s * SUB + k + 1], total.shape)
            for k in range(7)
        ]
        primal_square, dual_square, require_dot, objective_dot, bound_sum = line[:5]
        require_square, objective_square = line[5:]
        dual_value = require_dot + bound_sum
        primal_ratio = jnp.sqrt(primal_square) / (1.0 + jnp.sqrt(require_square))
        dual_ratio = jnp.sqrt(dual_square) / (1.0 + jnp.sqrt(objective_square))
        gap = jnp.abs(objective_dot - dual_value) / (
            1.0 + jnp.abs(objective_dot) + jnp.abs(dual_value)
        )
        lane = lax.broadcasted_iota(jnp.int32, primal_ratio.shape, 1)
        lines.append(jnp.where(lane == 0, primal_ratio, jnp.where(lane == 1, dual_ratio, gap)))
    out_ref[...] = jnp.concatenate(lines, 0)[:, : out_ref.shape[1]]


def restart_check(
    matrix_tiles,
    tile_rows,
    tile_columns,
    tile_counts,
    primal_iter,
    dual_iter,
    requirement,
    constraint_kind,
    objective,
    lower_bound,
    upper_bound,
    variable_kind,
    *,
    row_devices,
    col_devices,
):
    slot_count = matrix_tiles.shape[2]
    block_size = matrix_tiles.shape[-1]
    candidates, row_share = dual_iter.shape
    column_share = primal_iter.shape[1]
    row_steps = plain(row_devices)
    col_steps = crossed(col_devices)
    smem = pl.BlockSpec(memory_space=pltpu.SMEM)
    vmem = pl.BlockSpec(memory_space=pltpu.VMEM)
    hbm = pl.BlockSpec(memory_space=pltpu.HBM)
    primal_own, dual_own = pl.pallas_call(
        stage_kernel,
        name="stage",
        in_specs=[hbm] * 2,
        out_specs=[vmem] * 2,
        out_shape=[
            jax.ShapeDtypeStruct(primal_iter.shape, F32),
            jax.ShapeDtypeStruct(dual_iter.shape, F32),
        ],
        scratch_shapes=[pltpu.SemaphoreType.DMA((2,))],
        compiler_params=pltpu.CompilerParams(vmem_limit_bytes=4 << 20),
    )(in_hbm(primal_iter), in_hbm(dual_iter))
    primal_group, primal_send, primal_order = primal_own[None], primal_iter[None], [0]
    dual_group, dual_send, dual_order = dual_own[None], dual_iter[None], [0]
    gather_steps = col_steps[1:] + col_steps[:1]
    for step in range(max(len(row_steps), len(col_steps))):
        if step + 1 < len(row_steps):
            bit = row_steps[step]
            primal_send = gather_step(primal_group, primal_send, "row", bit, row_devices)
            primal_group, primal_order = primal_send, primal_order + [r ^ bit for r in primal_order]
        elif step < len(row_steps):
            bit = row_steps[step]
            primal_far = swap(primal_group, "row", bit, row_devices)
            primal_order = primal_order + [r ^ bit for r in primal_order]
        if step + 1 < len(col_steps):
            bit = gather_steps[step]
            dual_send = gather_step(dual_group, dual_send, "col", bit, col_devices)
            dual_group, dual_order = dual_send, dual_order + [r ^ bit for r in dual_order]
        elif step < len(col_steps):
            bit = gather_steps[step]
            dual_far = swap(dual_group, "col", bit, col_devices)
            dual_order = dual_order + [r ^ bit for r in dual_order]

    early = pl.pallas_call(
        early_kernel,
        name="early_tiles",
        in_specs=[hbm, vmem],
        out_specs=vmem,
        out_shape=jax.ShapeDtypeStruct((EARLY, block_size, block_size), F32),
        scratch_shapes=[pltpu.SemaphoreType.DMA((EARLY,))],
        compiler_params=pltpu.CompilerParams(vmem_limit_bytes=12 << 20),
    )(in_hbm(matrix_tiles), dual_group)

    extras = (
        (requirement, "col", row_share),
        (constraint_kind, "col", row_share),
        (objective, "row", column_share),
        (lower_bound, "row", column_share),
        (upper_bound, "row", column_share),
        (variable_kind, "row", column_share),
    )
    row_height = row_share // LANES
    column_height = column_share // LANES
    product_shape = (col_devices, candidates, row_height, LANES)
    transposed_shape = (row_devices, candidates, column_height, LANES)

    def half_of(shape):
        return jax.ShapeDtypeStruct((shape[0] // 2,) + shape[1:], F32)

    outs = pl.pallas_call(
        functools.partial(
            tile_kernel,
            slot_count=slot_count,
            block_size=block_size,
            row_devices=row_devices,
            col_devices=col_devices,
            row_share=row_share,
            column_share=column_share,
            extra_axes=tuple(axis for _, axis, _ in extras),
            primal_order=tuple(primal_order),
            dual_order=tuple(dual_order),
        ),
        name="tile_pass",
        in_specs=[smem] * 3
        + [hbm]
        + [vmem] * 5
        + [hbm] * len(extras),
        out_specs=[vmem] * (4 + len(extras)),
        out_shape=[half_of(product_shape)] * 2
        + [half_of(transposed_shape)] * 2
        + [
            jax.ShapeDtypeStruct((share // LANES, LANES), value.dtype)
            for value, _, share in extras
        ],
        scratch_shapes=[
            pltpu.VMEM((slot_count - EARLY, block_size, block_size), F32),
            pltpu.VMEM((row_devices, candidates, column_share), F32),
            pltpu.VMEM((col_devices, candidates, row_share), F32),
            pltpu.VMEM(product_shape, F32),
            pltpu.VMEM(transposed_shape, F32),
            pltpu.VMEM((LANES, block_size), F32),
            pltpu.VMEM((block_size, LANES), F32),
            pltpu.VMEM((slot_count, candidates, block_size, LANES), F32),
            pltpu.SemaphoreType.DMA((slot_count - EARLY,)),
            pltpu.SemaphoreType.DMA((len(extras),)),
        ],
        compiler_params=pltpu.CompilerParams(vmem_limit_bytes=32 << 20),
    )(
        in_hbm(tile_rows),
        in_hbm(tile_columns),
        tile_counts,
        in_hbm(matrix_tiles),
        early,
        primal_group,
        primal_far,
        dual_group,
        dual_far,
        *[in_hbm(value.reshape(-1, LANES)) for value, _, _ in extras],
    )
    product_keep, product_send, transposed_keep, transposed_send = outs[:4]
    for step in range(max(len(row_steps), len(col_steps))):
        if step < len(col_steps):
            product_got = swap(product_send, "col", col_steps[step], col_devices)
        if step < len(row_steps):
            transposed_got = swap(transposed_send, "row", row_steps[step], row_devices)
        if step + 1 < len(col_steps):
            half = product_keep.shape[0] // 2
            product_send = product_keep[half:] + product_got[half:]
            product_keep = product_keep[:half] + product_got[:half]
        if step + 1 < len(row_steps):
            half = transposed_keep.shape[0] // 2
            transposed_send = transposed_keep[half:] + transposed_got[half:]
            transposed_keep = transposed_keep[:half] + transposed_got[:half]

    devices = row_devices * col_devices
    primal_residual, dual_residual, stats = pl.pallas_call(
        side_kernel,
        name="sides",
        in_specs=[vmem] * 12,
        out_specs=[vmem] * 3,
        out_shape=[
            jax.ShapeDtypeStruct(dual_iter.shape, F32),
            jax.ShapeDtypeStruct(primal_iter.shape, F32),
            jax.ShapeDtypeStruct((devices, LANES), F32),
        ],
        compiler_params=pltpu.CompilerParams(vmem_limit_bytes=8 << 20),
    )(
        product_keep,
        product_got,
        transposed_keep,
        transposed_got,
        *outs[4:],
        primal_own,
        dual_own,
    )
    shared = lax.all_to_all(stats, ("row", "col"), 0, 0)
    metrics = pl.pallas_call(
        metric_kernel,
        name="metrics",
        in_specs=[vmem],
        out_specs=vmem,
        out_shape=jax.ShapeDtypeStruct((candidates, 3), F32),
        compiler_params=pltpu.CompilerParams(vmem_limit_bytes=8 << 20),
    )(shared)
    return (primal_residual, dual_residual, metrics)


def solution(mesh):
    placed = (
        P("row", "col", None, None, None),
        P("row", "col", None),
        P("row", "col", None),
        P("row", "col"),
        P(None, ("col", "row")),
        P(None, ("row", "col")),
        P("row"),
        P("row"),
        P("col"),
        P("col"),
        P("col"),
        P("col"),
    )
    return jax.shard_map(
        functools.partial(
            restart_check, row_devices=mesh.shape["row"], col_devices=mesh.shape["col"]
        ),
        mesh=mesh,
        in_specs=placed,
        out_specs=(P(None, ("row", "col")), P(None, ("col", "row")), P()),
        check_vma=False,
    )
```
